32 devices in a mesh: seq: 8 (over z, y), head: 4 (over x, core).
Axes of the slice: x: 2, y: 2, z: 4, core: 2. Of those that a mesh axis runs over, the one named last changes fastest.
Arguments:
- queries: bfloat16 [8192, 2048], P(('seq', 'head')), may hold values from -0.1875 to 0.1875
- key_rows: bfloat16 [8192, 2048], P(('seq', 'head')), may hold values from -1 to 1
- value_matrix: bfloat16 [8192, 2048], P(('seq', 'head')), may hold values from -1.75 to 1.75
- log_decay: bfloat16 [8192, 2048], P(('seq', 'head')), may hold values from -1 to 0, as said below
- beta_gate: bfloat16 [8192, 16], P(('seq', 'head')), may hold values from 0.19921875 to 1
- grad_out: bfloat16 [8192, 2048], P(('seq', 'head')), may hold values from -6 to 6
Outputs:
- grad_queries: bfloat16 [8192, 2048], P(('seq', 'head'))
- grad_keys: bfloat16 [8192, 2048], P(('seq', 'head'))
- grad_values: bfloat16 [8192, 2048], P(('seq', 'head'))
- grad_decay: bfloat16 [8192, 2048], P(('seq', 'head'))
- grad_beta: bfloat16 [8192, 16], P(('seq', 'head'))
The draws below stay inside these ranges and needn't reach their ends.
Inputs may be any that keep to these rules, and one draw needn't show every extreme that they name: `log_decay`: log decays are negative.
All inputs are finite; a program needn't handle non-finite values.
Results may differ from the reference program's by a relative error of at most 0.0095.
Values may be sent and summed in bfloat16 or wider, within the bound.
No kernel may reach another device: no remote copies, remote signals or barrier semaphores. Data moves between devices by JAX's collectives and lax.ppermute only.
A program may use at most 256 MiB of HBM per device.

```python
import math
import jax
import jax.numpy as jnp
from jax import lax

H = 16
DK = 128
DV = 128
SPAN = 64
SEQ = 8192


def draw_key_rows(key, part):
    columns = H * DK
    wide_count = max(DK * 3 // 8, 1)
    sub_keys = jax.random.split(key, 3)
    orders = jax.vmap(lambda head_key: jax.random.permutation(head_key, DK))(jax.random.split(sub_keys[0], H))
    wide = (orders < wide_count).reshape(columns)
    signs = (jax.random.randint(sub_keys[1], (columns,), 0, 2) * 2 - 1).astype(jnp.float32)
    fresh = jax.random.truncated_normal(sub_keys[2], -2.5, 2.5, (SEQ, columns), jnp.float32)
    wide_entries = (0.75 * signs[None, :] + 0.66 * fresh) / math.sqrt(wide_count)
    narrow_entries = fresh * math.sqrt(1.3 / SEQ)
    entries = jnp.where(wide[None, :], wide_entries, narrow_entries)
    return entries.astype(jnp.bfloat16)


def draw_log_decay(key, part):
    columns = H * DK
    sub_keys = jax.random.split(key, 7)
    slow_rate = jnp.exp(jax.random.uniform(sub_keys[0], (columns,), jnp.float32, math.log(0.05), math.log(1.2))) / SEQ
    fast_rate = jnp.exp(jax.random.uniform(sub_keys[1], (columns,), jnp.float32, math.log(1.0 / 50.0), math.log(1.0 / 30.0)))
    fast_share = 0.5
    chosen = jax.random.uniform(sub_keys[2], (columns,), jnp.float32) < fast_share
    rates = jnp.where(chosen, fast_rate, slow_rate)
    segment = jnp.arange(SEQ, dtype=jnp.int32) * 8 // SEQ
    factors = jnp.exp(jax.random.uniform(sub_keys[3], (8, columns), jnp.float32, math.log(0.5), math.log(2.0)))
    rough = jax.random.uniform(sub_keys[4], (SEQ, columns), jnp.float32, 0.5, 1.5)
    spots = jax.random.randint(sub_keys[5], (3,), 0, SEQ)
    struck = jnp.any(jnp.arange(SEQ, dtype=jnp.int32)[:, None] == spots[None, :], axis=1)
    depth = jax.random.uniform(sub_keys[6], (columns,), jnp.float32, 0.22, 0.69)
    entries = -(rates[None, :] * factors[segment] * rough) - jnp.where(struck[:, None], depth[None, :], 0.0)
    return entries.astype(jnp.bfloat16)


def shard_levels(rng, extent, cuts, least, largest):
    level = 1.0
    for dim, parts in cuts:
        draws = jax.random.uniform(jax.random.fold_in(jax.random.fold_in(rng, 6), dim), (parts,), jnp.float32, least / len(cuts), largest / len(cuts))
        level = level * jnp.repeat(jnp.exp(draws), extent[dim] // parts).reshape((-1,) + (1,) * (len(extent) - 1 - dim))
    return level


def normal_values(stream_key, extent, scale, reach, cuts=(), held_as=jnp.bfloat16):
    factor_of = shard_levels(stream_key, extent, cuts, -0.22, 0.18) if cuts else 1.0
    result = jax.random.normal(stream_key, extent, jnp.float32) * scale * factor_of
    return jnp.minimum(jnp.maximum(result, -reach), reach).astype(held_as)


def setup_inputs(seed: int = 0) -> dict:
    arg_keys = jax.random.split(jax.random.key(seed), 7)
    queries = normal_values(arg_keys[0], (SEQ, H * DK), 0.03, 0.1875, ((0, 32),))
    key_rows = draw_key_rows(jax.random.fold_in(arg_keys[6], 71), 0)
    value_matrix = normal_values(arg_keys[2], (SEQ, H * DV), 0.3, 1.75, ((0, 32),))
    log_decay = draw_log_decay(jax.random.fold_in(arg_keys[6], 71), 0)
    beta_gate = jnp.clip(0.19921875 + 0.80078125 * jax.random.uniform(arg_keys[4], (SEQ, H), jnp.float32) ** shard_levels(arg_keys[4], (SEQ, H), ((0, 32),), -0.2, 0.2), 0.19921875, 1.0).astype(jnp.bfloat16)
    grad_out = normal_values(arg_keys[5], (SEQ, H * DV), 1.0, 6.0, ((0, 32),))
    return dict(queries=queries, key_rows=key_rows, value_matrix=value_matrix, log_decay=log_decay, beta_gate=beta_gate, grad_out=grad_out)


PRECISE = lax.Precision.HIGHEST

def matrix_product(form, left, right):
    return jnp.einsum(form, left, right, precision=PRECISE)

def substitute(system):
    order_size = system.shape[-1]
    leading = system.shape[:-2]
    flattened = system.reshape((-1, order_size, order_size)).transpose(1, 2, 0)
    identity = jnp.eye(order_size, dtype=jnp.float32)
    found_rows = []
    for row_index in range(order_size):
        current = jnp.broadcast_to(identity[row_index][:, None], (order_size, flattened.shape[2]))
        if row_index > 0:
            earlier_rows = jnp.stack(found_rows)
            current = current - lax.optimization_barrier(jnp.sum(flattened[row_index, :row_index][:, None, :] * earlier_rows, axis=0))
        found_rows.append(current)
    return jnp.stack(found_rows).transpose(2, 0, 1).reshape(leading + (order_size, order_size))

def unit_lower_inverse(system):
    order_size = system.shape[-1]
    if order_size <= 16:
        return substitute(system)
    half_size = order_size // 2
    blocks = unit_lower_inverse(jnp.stack([system[..., :half_size, :half_size], system[..., half_size:, half_size:]]))
    upper_block = blocks[0]
    lower_block = blocks[1]
    corner = -matrix_product('...ij,...jk->...ik', lower_block, matrix_product('...ij,...jk->...ik', system[..., half_size:, :half_size], upper_block))
    top_rows = jnp.concatenate([upper_block, jnp.zeros_like(upper_block)], axis=-1)
    bottom_rows = jnp.concatenate([corner, lower_block], axis=-1)
    return jnp.concatenate([top_rows, bottom_rows], axis=-2)

def span_tables(queries, key_rows, decays, betas):
    length = decays.shape[-2]
    running = jnp.cumsum(decays, axis=-2)
    middle = running[..., length // 2:length // 2 + 1, :]
    ending = running[..., length - 1:, :]
    key_up = key_rows * jnp.exp(running - middle)
    key_down = key_rows * jnp.exp(middle - running)
    query_up = queries * jnp.exp(running - middle)
    row_ids = lax.broadcasted_iota(jnp.int32, (length, length), 0)
    col_ids = lax.broadcasted_iota(jnp.int32, (length, length), 1)
    key_pairs = matrix_product('...cd,...sd->...cs', key_up, key_down)
    scores = matrix_product('...cd,...sd->...cs', query_up, key_down)
    linear_system = jnp.where(row_ids > col_ids, key_pairs, 0.0) * betas[..., None, :] + jnp.eye(length, dtype=jnp.float32)
    reachability_table = jnp.where(row_ids >= col_ids, scores, 0.0) * betas[..., None, :]
    key_offset = key_rows * jnp.exp(running)
    query_offset = queries * jnp.exp(running)
    last_key = key_rows * jnp.exp(ending - running) * betas[..., :, None]
    return (unit_lower_inverse(linear_system), reachability_table, key_offset, query_offset, last_key, jnp.exp(ending[..., 0, :]))

def span_apply(carried_state, pieces):
    queries, key_rows, value_matrix, decays, betas = pieces
    inverse, reachability_table, key_offset, query_offset, last_key, final_decay = span_tables(queries, key_rows, decays, betas)
    written_state = matrix_product('...cs,...sv->...cv', inverse, value_matrix - matrix_product('...cm,...mv->...cv', key_offset, carried_state))
    output_rows = matrix_product('...cm,...mv->...cv', query_offset, carried_state) + matrix_product('...cs,...sv->...cv', reachability_table, written_state)
    carried_state = final_decay[..., :, None] * carried_state + matrix_product('...ck,...cv->...kv', last_key, written_state)
    return (carried_state, output_rows)

def run_spans(pieces, initial):
    ending, outputs = lax.scan(jax.checkpoint(span_apply), initial, pieces)
    return (outputs, ending)

def reference(queries, key_rows, value_matrix, log_decay, beta_gate, grad_out):
    spans = SEQ // SPAN
    member = math.gcd(H, 8)
    groups = H // member

    def arrange(source, columns):
        return source.astype(jnp.float32).reshape(spans, SPAN, groups, member, columns).transpose(2, 0, 3, 1, 4)

    def per_group(members):
        query_part, key_part, value_part, decay_part, beta_part, output_part = members
        initial = jnp.zeros((member, DK, DV), jnp.float32)

        def forward(query_input, key_input, value_input, decay_input, beta_input):
            return run_spans((query_input, key_input, value_input, decay_input, beta_input), initial)
        (outputs, ending), pull_back = jax.vjp(forward, query_part, key_part, value_part, decay_part, beta_part)
        return pull_back((output_part, jnp.zeros_like(ending)))
    betas = beta_gate.astype(jnp.float32).reshape(spans, SPAN, groups, member).transpose(2, 0, 3, 1)
    gradients = lax.map(per_group, (arrange(queries, DK), arrange(key_rows, DK), arrange(value_matrix, DV), arrange(log_decay, DK), betas, arrange(grad_out, DV)))

    def restore(source, columns):
        return source.transpose(1, 3, 0, 2, 4).reshape(SEQ, H * columns).astype(jnp.bfloat16)
    grad_beta = gradients[4].transpose(1, 3, 0, 2).reshape(SEQ, H).astype(jnp.bfloat16)
    return (restore(gradients[0], DK), restore(gradients[1], DK), restore(gradients[2], DV), restore(gradients[3], DK), grad_beta)
```

```python
import functools

import jax
import jax.numpy as jnp
from jax import lax
from jax.experimental import pallas as pl
from jax.experimental.pallas import tpu as pltpu
from jax.sharding import PartitionSpec as P

DK = 128
DV = 128
SPAN = 128
ROWS = 3 * DK + 16
F32 = jnp.float32
BF16 = jnp.bfloat16


def split(x):
    if isinstance(x, tuple):
        return x
    if x.dtype == BF16:
        return (x, None)
    high = x.astype(BF16)
    return (high, (x - high.astype(F32)).astype(BF16))


def product(left, right, left_dim, right_dim):
    left_high, left_low = split(left)
    right_high, right_low = split(right)
    lefts, rights = [left_high], [right_high]
    if left_low is not None:
        lefts.append(left_low)
        rights.append(right_high)
    if right_low is not None:
        lefts.append(left_high)
        rights.append(right_low)
    if len(lefts) > 1:
        left_all = jnp.concatenate(lefts, axis=left_dim)
        right_all = jnp.concatenate(rights, axis=right_dim)
    else:
        left_all, right_all = left_high, right_high
    return lax.dot_general(
        left_all, right_all, (((left_dim,), (right_dim,)), ((), ())), preferred_element_type=F32
    )


def nn(left, right):
    return product(left, right, 1, 0)


def nt(left, right):
    return product(left, right, 1, 1)


def tn(left, right):
    return product(left, right, 0, 0)


def iotas(n=SPAN):
    return (
        lax.broadcasted_iota(jnp.int32, (n, n), 0),
        lax.broadcasted_iota(jnp.int32, (n, n), 1),
    )


def diagonal(row):
    rows, cols = iotas()
    return jnp.where(rows == cols, row, 0.0)


def column(row):
    return jnp.sum(diagonal(row), axis=1, keepdims=True)


def unit_lower_inverses(strict):
    rows, cols = iotas()
    unit = jnp.where(rows == cols, 1.0, 0.0)
    found = None
    size = 1
    while size < SPAN:
        inside = (
            (rows // (2 * size) == cols // (2 * size))
            & ((rows // size) % 2 == 1)
            & ((cols // size) % 2 == 0)
        )
        corners = [jnp.where(inside, n, 0.0) for n in strict]
        if found is None:
            found = [unit - c for c in corners]
        else:
            parts = [split(x) for x in found]
            inner = [nn(c, x) for c, x in zip(corners, parts)]
            found = [x - nn(p, i) for x, p, i in zip(found, parts, inner)]
        size *= 2
    return found


def span_tables(q, k, g, beta):
    rows, cols = iotas()
    lower = jnp.where(rows >= cols, 1.0, 0.0).astype(BF16)
    running = nn(lower, g)
    middle = running[SPAN // 2 : SPAN // 2 + 1, :]
    ending = running[SPAN - 1 : SPAN, :]
    up = jnp.exp(running - middle)
    down = jnp.exp(middle - running)
    start_factor = jnp.exp(middle)
    end_factor = jnp.exp(ending - middle)
    k = k.astype(F32)
    key_up = k * up
    query_up = q.astype(F32) * up
    key_down = k * down
    key_write = key_down * beta
    return dict(
        up=up,
        down=down,
        start_factor=start_factor,
        end_factor=end_factor,
        final=jnp.exp(ending),
        key_up=key_up,
        query_up=query_up,
        key_down=key_down,
        key_write=key_write,
        key_offset=key_up * start_factor,
        query_offset=query_up * start_factor,
        key_end=key_write * end_factor,
    )


def head_betas(beta_ref, head):
    heads = beta_ref.shape[1]
    picked = jnp.where(
        lax.broadcasted_iota(jnp.int32, (heads, DK), 0) == head, 1.0, 0.0
    ).astype(BF16)
    return nn(beta_ref[...], picked)


def block_kernel(batch, me_ref, q_ref, k_ref, v_ref, g_ref, do_ref, beta_ref, msg_ref, ux_ref, ar_ref):
    del me_ref
    step = pl.program_id(0)
    spans = q_ref.shape[0] // SPAN
    rows, cols = iotas()
    places = [(h, n) for h in range(batch) for n in range(spans)]
    betas = [head_betas(beta_ref, step * batch + h) for h in range(batch)]
    tables, strict, reach = {}, {}, {}
    for h, n in places:
        at = (slice(n * SPAN, (n + 1) * SPAN), slice(h * DK, (h + 1) * DK))
        t = span_tables(q_ref[at], k_ref[at], g_ref[at], betas[h][at[0]])
        both = nt(jnp.concatenate([t["key_up"], t["query_up"]], axis=0), t["key_write"])
        strict[h, n] = jnp.where(rows > cols, both[:SPAN], 0.0)
        reach[h, n] = jnp.where(rows >= cols, both[SPAN:], 0.0)
        tables[h, n] = t
    inverses = dict(zip(places, unit_lower_inverses([strict[p] for p in places])))
    solved = {}
    for h, n in places:
        at = (slice(n * SPAN, (n + 1) * SPAN), slice(h * DK, (h + 1) * DK))
        ar_ref[at[0], h * 2 * SPAN : h * 2 * SPAN + SPAN] = inverses[h, n]
        ar_ref[at[0], h * 2 * SPAN + SPAN : (h + 1) * 2 * SPAN] = reach[h, n]
        inverse = split(inverses[h, n])
        solved[h, n] = (nn(inverse, tables[h, n]["key_offset"]), nn(inverse, v_ref[at]))
    state, read = {}, {}
    for n in range(spans):
        for h in range(batch):
            t = tables[h, n]
            across, own = solved[h, n]
            reach_parts = split(reach[h, n])
            at = slice(n * SPAN, (n + 1) * SPAN)
            if n == 0:
                ux = jnp.concatenate([-across, own], axis=1)
                out_map = t["query_offset"] + nn(reach_parts, ux[:, :DK])
                kept = jnp.concatenate([diagonal(t["final"]), jnp.zeros((DK, DV), F32)], axis=1)
            else:
                parts = split(state[h])
                moved = nn(across, parts)
                ux = jnp.concatenate([-moved[:, :DK], own - moved[:, DK:]], axis=1)
                out_map = nn(t["query_offset"], (parts[0][:, :DK], parts[1][:, :DK])) + nn(
                    reach_parts, ux[:, :DK]
                )
                kept = column(t["final"]) * state[h]
            ux_ref[at, h * 2 * DK : (h + 1) * 2 * DK] = ux
            state[h] = kept + tn(t["key_end"], ux)
            term = tn(out_map, do_ref[at, h * DV : (h + 1) * DV])
            read[h] = term if n == 0 else read[h] + term
    for h in range(batch):
        store_message(msg_ref, h, state[h][:, :DK], state[h][:, DK:], read[h])


def store_message(msg_ref, h, block_map, shift, read):
    rows, cols = iotas()
    rounded = block_map.astype(BF16)
    left = jnp.where(rows == cols, block_map - rounded.astype(F32), 0.0)
    msg_ref[h, 0:DK, :] = rounded
    msg_ref[h, DK : 2 * DK, :] = shift.astype(BF16)
    msg_ref[h, 2 * DK : 3 * DK, :] = read.astype(BF16)
    msg_ref[h, 3 * DK :, :] = jnp.broadcast_to(
        jnp.sum(left, axis=0, keepdims=True), (16, DK)
    ).astype(BF16)


def load_map(ref, *at):
    rows, cols = iotas()
    row = ref[at + (slice(3 * DK, ROWS), slice(None))][0:1, :].astype(F32)
    return (
        ref[at + (slice(0, DK), slice(None))],
        jnp.where(rows == cols, row, 0.0).astype(BF16),
    )


def load_shift(ref, *at):
    return ref[at + (slice(DK, 2 * DK), slice(None))]


def load_read(ref, *at):
    return ref[at + (slice(2 * DK, 3 * DK), slice(None))]


def whole_map(parts):
    return parts[0].astype(F32) + parts[1].astype(F32)


def backward_kernel(batch, q_ref, k_ref, g_ref, do_ref, beta_ref, ar_ref, wx_ref):
    step = pl.program_id(0)
    spans = q_ref.shape[0] // SPAN
    betas = [head_betas(beta_ref, step * batch + h) for h in range(batch)]
    carried = {}
    for n in range(spans - 1, -1, -1):
        for h in range(batch):
            at = (slice(n * SPAN, (n + 1) * SPAN), slice(h * DK, (h + 1) * DK))
            t = span_tables(q_ref[at], k_ref[at], g_ref[at], betas[h][at[0]])
            do = do_ref[at]
            inverse = split(ar_ref[at[0], h * 2 * SPAN : h * 2 * SPAN + SPAN])
            reach = ar_ref[at[0], h * 2 * SPAN + SPAN : (h + 1) * 2 * SPAN]
            own = tn(inverse, tn(reach, do))
            through = tn(inverse, t["key_end"])
            if n == spans - 1:
                wx = jnp.concatenate([through, own], axis=1)
            else:
                moved = nn(through, carried[h])
                wx = jnp.concatenate([moved[:, :DK], moved[:, DK:] + own], axis=1)
            wx_ref[at[0], h * 2 * DK : (h + 1) * 2 * DK] = wx
            if n > 0:
                read = tn(t["query_offset"], do)
                if n == spans - 1:
                    kept = jnp.concatenate([diagonal(t["final"]), read], axis=1)
                else:
                    kept = column(t["final"]) * carried[h]
                    kept = jnp.concatenate([kept[:, :DK], kept[:, DK:] + read], axis=1)
                carried[h] = kept - tn(t["key_offset"], wx)


def compose_kernel(me_ref, parts_ref, total_ref):
    me = me_ref[0]
    count, heads = parts_ref.shape[:2]
    for h in range(heads):
        first = load_map(parts_ref, me, h)
        state = jnp.concatenate([whole_map(first), load_shift(parts_ref, me, h).astype(F32)], axis=1)
        for j in range(1, count):
            at = jnp.bitwise_xor(me, j)
            moved = nn(load_map(parts_ref, at, h), state)
            state = jnp.concatenate(
                [moved[:, :DK], moved[:, DK:] + load_shift(parts_ref, at, h).astype(F32)], axis=1
            )
        read = load_read(parts_ref, jnp.bitwise_xor(me, count - 1), h).astype(F32)
        for j in range(count - 2, -1, -1):
            at = jnp.bitwise_xor(me, j)
            read = tn(load_map(parts_ref, at, h), read) + load_read(parts_ref, at, h).astype(F32)
        store_message(total_ref, h, state[:, :DK], state[:, DK:], read)


def join_kernel(first, last, upper_ref, own_ref, other_ref, carry_ref, total_ref, next_ref):
    heads = own_ref.shape[0]
    rows, cols = iotas()
    unit = jnp.where(rows == cols, 1.0, 0.0)

    def part(i):
        return slice(i * DK, (i + 1) * DK)

    @pl.when(upper_ref[0] == 1)
    def _():
        for h in range(heads):
            early = load_map(other_ref, h)
            shift = load_shift(other_ref, h)
            if first:
                next_ref[h, part(1)] = shift.astype(F32)
                next_ref[h, part(2)] = jnp.zeros((DK, DV), F32)
                next_ref[h, part(0)] = whole_map(early)
                next_ref[h, part(3)] = unit
            else:
                before = carry_ref[h, part(0)]
                next_ref[h, part(1)] = nn(before, shift) + carry_ref[h, part(1)]
                next_ref[h, part(2)] = carry_ref[h, part(2)]
                if not last:
                    next_ref[h, part(0)] = nn(before, early)
                    next_ref[h, part(3)] = carry_ref[h, part(3)]
            if not last:
                late = load_map(own_ref, h)
                store_message(
                    total_ref,
                    h,
                    nn(late, early),
                    nn(late, shift) + load_shift(own_ref, h).astype(F32),
                    load_read(other_ref, h).astype(F32) + tn(early, load_read(own_ref, h)),
                )

    @pl.when(upper_ref[0] == 0)
    def _():
        for h in range(heads):
            late = load_map(other_ref, h)
            read = load_read(other_ref, h)
            if first:
                next_ref[h, part(1)] = jnp.zeros((DK, DV), F32)
                next_ref[h, part(2)] = read.astype(F32)
                next_ref[h, part(0)] = unit
                next_ref[h, part(3)] = whole_map(late)
            else:
                after = carry_ref[h, part(3)]
                next_ref[h, part(2)] = tn(after, read) + carry_ref[h, part(2)]
                next_ref[h, part(1)] = carry_ref[h, part(1)]
                if not last:
                    next_ref[h, part(3)] = nn(late, after)
                    next_ref[h, part(0)] = carry_ref[h, part(0)]
            if not last:
                early = load_map(own_ref, h)
                store_message(
                    total_ref,
                    h,
                    nn(late, early),
                    nn(late, load_shift(own_ref, h)) + load_shift(other_ref, h).astype(F32),
                    load_read(own_ref, h).astype(F32) + tn(early, read),
                )


def spread_kernel(me_ref, parts_ref, carry_ref, out_ref):
    me = me_ref[0]
    count, heads = parts_ref.shape[:2]
    for h in range(heads):
        state = carry_ref[h, DK : 2 * DK]
        for j in range(count):
            at = jnp.bitwise_xor(me, j)
            out_ref[at, h, 0:DK] = state.astype(BF16)
            if j < count - 1:
                state = nn(load_map(parts_ref, at, h), state) + load_shift(parts_ref, at, h).astype(F32)
        grad = carry_ref[h, 2 * DK : 3 * DK]
        for j in range(count - 1, -1, -1):
            at = jnp.bitwise_xor(me, j)
            out_ref[at, h, DK:] = grad.astype(BF16)
            if j > 0:
                grad = tn(load_map(parts_ref, at, h), grad) + load_read(parts_ref, at, h).astype(F32)


def gradient_kernel(
    batch, me_ref, q_ref, k_ref, g_ref, do_ref, beta_ref, ux_ref, wx_ref, ends_ref,
    dq_ref, dk_ref, dv_ref, dg_ref, db_ref,
):
    del me_ref
    step = pl.program_id(0)
    tokens = q_ref.shape[0]
    spans = tokens // SPAN
    rows, cols = iotas()
    upper = jnp.where(rows <= cols, 1.0, 0.0).astype(BF16)
    ones = jnp.ones((8, DV), BF16)
    lanes = lax.broadcasted_iota(jnp.int32, (tokens, beta_ref.shape[1]), 1)

    @pl.when(step == 0)
    def _():
        db_ref[...] = jnp.zeros_like(db_ref)

    all_gates = db_ref[...]
    for h in range(batch):
        head = step * batch + h
        beta = head_betas(beta_ref, head)
        wide = slice(h * DK, (h + 1) * DK)
        start = ends_ref[0, h, 0:DK]
        end = ends_ref[0, h, DK:]
        ux = ux_ref[:, h * 2 * DK : (h + 1) * 2 * DK]
        wx = wx_ref[:, h * 2 * DK : (h + 1) * 2 * DK]
        written = ux[:, DK:] + nn(ux[:, :DK], start)
        grad_write = wx[:, DK:] + nn(wx[:, :DK], end)
        dv_ref[:, wide] = grad_write.astype(BF16)
        tables, us, lefts = [], [], []
        for n in range(spans):
            at = slice(n * SPAN, (n + 1) * SPAN)
            tables.append(span_tables(q_ref[at, wide], k_ref[at, wide], g_ref[at, wide], beta[at]))
            us.append(split(written[at]))
            high, low = split(-grad_write[at])
            do = do_ref[at, wide]
            lefts.append((high, low, do))
        states, grads = [start], [None] * spans
        state = start.astype(F32)
        for n in range(spans - 1):
            state = column(tables[n]["final"]) * state + tn(tables[n]["key_end"], us[n])
            states.append(split(state))
        grads[spans - 1] = end
        grad = end.astype(F32)
        for n in range(spans - 1, 0, -1):
            high, low, do = lefts[n]
            grad = (
                column(tables[n]["final"]) * grad
                + tn(tables[n]["query_offset"], do)
                + tn(tables[n]["key_offset"], (high, low))
            )
            grads[n - 1] = split(grad)
        gates = []
        for n in range(spans):
            at = slice(n * SPAN, (n + 1) * SPAN)
            t = tables[n]
            high, low, do = lefts[n]
            left = (
                jnp.concatenate([high, do], axis=0),
                jnp.concatenate([low, jnp.zeros_like(low)], axis=0),
            )
            from_state = nt(left, states[n])
            pairs = nt(left, us[n])
            grad_end = nt(us[n], grads[n])
            pairs = jnp.concatenate(
                [jnp.where(rows > cols, pairs[:SPAN], 0.0), jnp.where(rows >= cols, pairs[SPAN:], 0.0)],
                axis=0,
            )
            pairs = split(pairs)
            ups = nn(pairs, t["key_write"])
            key_up_grad = ups[:SPAN] + from_state[:SPAN] * t["start_factor"]
            query_up_grad = ups[SPAN:] + from_state[SPAN:] * t["start_factor"]
            write_grad = (
                tn(pairs, jnp.concatenate([t["key_up"], t["query_up"]], axis=0))
                + grad_end * t["end_factor"]
            )
            dq_ref[at, wide] = (query_up_grad * t["up"]).astype(BF16)
            dk_ref[at, wide] = (key_up_grad * t["up"] + write_grad * t["down"] * beta[at]).astype(BF16)
            gates.append(jnp.sum(write_grad * t["key_down"], axis=1, keepdims=True))
            flow = query_up_grad * t["query_up"] + key_up_grad * t["key_up"] - write_grad * t["key_write"]
            span_state = whole(states[n])
            span_grad = whole(grads[n])
            last = jnp.sum(grad_end * t["key_end"], axis=0, keepdims=True) + t["final"] * nt(
                ones, span_state * span_grad
            )[0:1]
            dg_ref[at, wide] = (nn(upper, flow) + last).astype(BF16)
        gate = jnp.concatenate(gates, axis=0)
        all_gates = jnp.where(lanes == head, gate, all_gates.astype(F32)).astype(BF16)
    db_ref[...] = all_gates


def whole(x):
    if isinstance(x, tuple):
        return x[0].astype(F32) + x[1].astype(F32)
    return x.astype(F32)


def params(semantics=("arbitrary",)):
    return pltpu.CompilerParams(dimension_semantics=semantics, vmem_limit_bytes=56 << 20)


def cost(flops, data):
    return pl.CostEstimate(flops=int(flops), bytes_accessed=int(data), transcendentals=0)


def local(queries, key_rows, value_matrix, log_decay, beta_gate, grad_out):
    tokens, heads = beta_gate.shape
    count = lax.axis_size("head")
    blocks = lax.axis_size("seq")
    mine = heads // count
    batch = 2 if mine % 2 == 0 else 1
    per = mine // batch
    steps = heads // batch
    me = lax.axis_index("head").astype(jnp.int32)
    place = lax.axis_index("seq").astype(jnp.int32)
    me_row = me.reshape(1)
    flops = 2 * 3 * steps * batch * tokens * DK * DK

    def wide(columns):
        return pl.BlockSpec((tokens, batch * columns), lambda i, *_: (0, i))

    beta_spec = pl.BlockSpec((tokens, heads), lambda i, *_: (0, 0))

    def ordered(rows):
        return pl.BlockSpec(
            (None, batch, rows, DK),
            lambda i, m: (jnp.bitwise_xor(i // per, m[0]), i % per, 0, 0),
        )

    messages, ux, ar = pl.pallas_call(
        functools.partial(block_kernel, batch),
        grid_spec=pltpu.PrefetchScalarGridSpec(
            num_scalar_prefetch=1,
            grid=(steps,),
            in_specs=[wide(DK), wide(DK), wide(DV), wide(DK), wide(DV), beta_spec],
            out_specs=[ordered(ROWS), wide(2 * DK), wide(2 * SPAN)],
        ),
        out_shape=[
            jax.ShapeDtypeStruct((count, mine, ROWS, DK), BF16),
            jax.ShapeDtypeStruct((tokens, heads * 2 * DK), F32),
            jax.ShapeDtypeStruct((tokens, heads * 2 * SPAN), F32),
        ],
        compiler_params=params(),
        cost_estimate=cost(24 * flops, 20 << 20),
        name="block_maps",
    )(me_row, queries, key_rows, value_matrix, log_decay, grad_out, beta_gate)

    def exchange(parts):
        return jnp.stack(
            [parts[0]]
            + [
                lax.ppermute(parts[d], "head", [(i, i ^ d) for i in range(count)])
                for d in range(1, count)
            ]
        )

    gathered = exchange(messages)

    wx = pl.pallas_call(
        functools.partial(backward_kernel, batch),
        grid_spec=pltpu.PrefetchScalarGridSpec(
            num_scalar_prefetch=0,
            grid=(steps,),
            in_specs=[wide(DK), wide(DK), wide(DK), wide(DV), beta_spec, wide(2 * SPAN)],
            out_specs=wide(2 * DK),
        ),
        out_shape=jax.ShapeDtypeStruct((tokens, heads * 2 * DK), F32),
        compiler_params=params(),
        cost_estimate=cost(8 * flops, 12 << 20),
        name="backward_maps",
    )(queries, key_rows, log_decay, grad_out, beta_gate, ar)

    smem = pl.BlockSpec(memory_space=pltpu.SMEM)
    vmem = pl.BlockSpec(memory_space=pltpu.VMEM)
    total_shape = jax.ShapeDtypeStruct((mine, ROWS, DK), BF16)
    carry_shape = jax.ShapeDtypeStruct((mine, 4 * DK, DK), F32)
    total = pl.pallas_call(
        compose_kernel,
        in_specs=[smem, vmem],
        out_specs=vmem,
        out_shape=total_shape,
        compiler_params=pltpu.CompilerParams(vmem_limit_bytes=40 << 20),
        name="compose",
    )(me_row, gathered)
    carry = jnp.zeros(carry_shape.shape, F32)
    distance = 1
    while distance < blocks:
        first, last = distance == 1, 2 * distance >= blocks
        other = lax.ppermute(total, "seq", [(i, i ^ distance) for i in range(blocks)])
        upper = (jnp.bitwise_and(place, distance) != 0).astype(jnp.int32).reshape(1)
        total, carry = pl.pallas_call(
            functools.partial(join_kernel, first, last),
            in_specs=[smem, vmem, vmem, vmem],
            out_specs=[vmem, vmem],
            out_shape=[total_shape, carry_shape],
            compiler_params=pltpu.CompilerParams(vmem_limit_bytes=40 << 20),
            name="join",
        )(upper, total, other, carry)
        distance *= 2
    ends = pl.pallas_call(
        spread_kernel,
        in_specs=[smem, vmem, vmem],
        out_specs=vmem,
        out_shape=jax.ShapeDtypeStruct((count, mine, 2 * DK, DV), BF16),
        compiler_params=pltpu.CompilerParams(vmem_limit_bytes=40 << 20),
        name="spread",
    )(me_row, gathered, carry)
    ends = exchange(ends)

    token_shape = jax.ShapeDtypeStruct(queries.shape, BF16)
    return pl.pallas_call(
        functools.partial(gradient_kernel, batch),
        grid_spec=pltpu.PrefetchScalarGridSpec(
            num_scalar_prefetch=1,
            grid=(steps,),
            in_specs=[
                wide(DK), wide(DK), wide(DK), wide(DV), beta_spec, wide(2 * DK), wide(2 * DK),
                pl.BlockSpec(
                    (1, batch, 2 * DK, DV),
                    lambda i, m: (jnp.bitwise_xor(i // per, m[0]), i % per, 0, 0),
                ),
            ],
            out_specs=[wide(DK), wide(DK), wide(DV), wide(DK), beta_spec],
        ),
        out_shape=[
            token_shape, token_shape, token_shape, token_shape,
            jax.ShapeDtypeStruct(beta_gate.shape, BF16),
        ],
        compiler_params=params(),
        cost_estimate=cost(16 * flops, 20 << 20),
        name="gradients",
    )(me_row, queries, key_rows, log_decay, grad_out, beta_gate, ux, wx, ends)


def solution(mesh):
    spec = P(("seq", "head"), None)
    return jax.shard_map(
        lambda *arrays: tuple(local(*arrays)),
        mesh=mesh,
        in_specs=(spec,) * 6,
        out_specs=(spec,) * 5,
        check_vma=False,
    )
```

```python
import functools

import jax
import jax.numpy as jnp
import numpy as np
from jax import lax
from jax.experimental import pallas as pl
from jax.experimental.pallas import tpu as pltpu
from jax.sharding import PartitionSpec as P

DK = 128
DV = 128
SPAN = 128
STRIP = 16
ROWS = 3 * DK + 16
F32 = jnp.float32
BF16 = jnp.bfloat16


def split(x):
    if isinstance(x, tuple):
        return x
    if x.dtype == BF16:
        return (x, None)
    high = x.astype(BF16)
    return (high, (x - high.astype(F32)).astype(BF16))


def product(left, right, left_dim, right_dim, stacked=True):
    left_high, left_low = split(left)
    right_high, right_low = split(right)
    columns = right_high.shape[1 - right_dim]
    lefts, rights = [left_high], [right_high]
    wide = (
        left_low is not None
        and right_low is not None
        and columns <= DK
        and stacked
    )
    if wide:
        both = jnp.concatenate([right_high, right_low], axis=1 - right_dim)
        lefts, rights = [left_high, left_low], [both, both]
    else:
        if left_low is not None:
            lefts.append(left_low)
            rights.append(right_high)
        if right_low is not None:
            lefts.append(left_high)
            rights.append(right_low)
    left_all, right_all = lefts[0], rights[0]
    if len(lefts) > 1:
        left_all = jnp.concatenate(lefts, axis=left_dim)
        right_all = jnp.concatenate(rights, axis=right_dim)
    found = lax.dot_general(
        left_all, right_all, (((left_dim,), (right_dim,)), ((), ())), preferred_element_type=F32
    )
    return found[:, :columns] + found[:, columns:] if wide else found


def nn(left, right):
    return product(left, right, 1, 0)


def nt(left, right):
    return product(left, right, 1, 1)


def tn(left, right, stacked=False):
    return product(left, right, 0, 0, stacked)


def iotas(n=SPAN):
    return (
        lax.broadcasted_iota(jnp.int32, (n, n), 0),
        lax.broadcasted_iota(jnp.int32, (n, n), 1),
    )


def diagonal(row):
    rows, cols = iotas()
    return jnp.where(rows == cols, row, 0.0)


def column(row):
    return jnp.sum(diagonal(row), axis=1, keepdims=True)


def strip_map(fn, rows=SPAN):
    found = [fn(slice(i, i + STRIP)) for i in range(0, rows, STRIP)]
    return tuple(jnp.concatenate(parts, axis=0) for parts in zip(*found))


def split_strips(x):
    return strip_map(lambda at: split(x[at]), x.shape[0])


def level_masks():
    rows = np.arange(SPAN)[:, None]
    cols = np.arange(SPAN)[None, :]
    masks, size = [], 1
    while size < SPAN:
        masks.append((rows // size % 2 == 1) & (rows // size == cols // size + 1))
        size *= 2
    return jnp.asarray(np.stack(masks), BF16)


def unit_lower_inverses(strict, mask_ref):
    rows, cols = iotas()
    unit = jnp.where(rows == cols, 1.0, 0.0)
    mask = mask_ref[0].astype(F32)
    found = [strip_map(lambda at, n=n: whole_and_split(unit[at] - n[0][at] * mask[at])) for n in strict]
    strict = [(n[1], n[2]) for n in strict]
    for level in range(1, mask_ref.shape[0]):
        mask = mask_ref[level]
        inner = [split_strips(nn((n[0] * mask, n[1] * mask), x[1:])) for n, x in zip(strict, found)]
        outer = [nn(x[1:], i) for i, x in zip(inner, found)]
        found = [
            strip_map(lambda at, x=x, o=o: whole_and_split(x[0][at] - o[at])) for x, o in zip(found, outer)
        ]
    return [x[1:] for x in found]


def whole_and_split(x):
    return (x,) + split(x)


def decays(g):
    rows, cols = iotas()
    lower = jnp.where(rows >= cols, 1.0, 0.0).astype(BF16)
    running = nn(lower, g)
    middle = running[SPAN // 2 : SPAN // 2 + 1, :]
    ending = running[SPAN - 1 : SPAN, :]
    return running, middle, jnp.exp(middle), jnp.exp(ending - middle), jnp.exp(ending)


def head_betas(beta_ref, head):
    heads = beta_ref.shape[0]
    picked = jnp.where(
        lax.broadcasted_iota(jnp.int32, (heads, DK), 0) == head, 1.0, 0.0
    ).astype(BF16)
    return tn(beta_ref[...], picked)


class Side:
    def __init__(self, refs):
        self.refs, self.width = refs, refs[0].shape[1]
        self.shape = (refs[0].shape[0], self.width * len(refs))

    def __getitem__(self, at):
        rows, columns = at
        i = columns.start // self.width
        return self.refs[i][rows, columns.start - i * self.width : columns.stop - i * self.width]


def block_kernel(batch, groups, group, pair, me_ref, *refs):
    q_ref, k_ref, v_ref, g_ref, do_ref = [Side(refs[i * pair : (i + 1) * pair]) for i in range(5)]
    beta_ref, mask_ref, msg_ref, um_ref, ub_ref, ar_ref = refs[5 * pair :]
    swapped = jnp.bitwise_and(me_ref[0], pair - 1)
    first = pl.program_id(0) * pair
    own, batch = batch, pair * batch
    spans = q_ref.shape[0] // SPAN
    rows, cols = iotas()
    places = [(h, n) for h in range(batch) for n in range(spans)]
    betas = [
        head_betas(beta_ref, ((first + h // own) * groups + group) * own + h % own) for h in range(batch)
    ]
    tables, strict, reach, finals = {}, {}, {}, {}
    for h, n in places:
        base = n * SPAN
        wide = slice(h * DK, (h + 1) * DK)
        running, middle, start_factor, end_factor, final = decays(g_ref[base : base + SPAN, wide])
        finals[h, n] = final

        def table(at):
            of = slice(base + at.start, base + at.stop)
            up = jnp.exp(running[at] - middle)
            down = jnp.exp(middle - running[at])
            k = k_ref[of, wide].astype(F32)
            key_up = k * up
            query_up = q_ref[of, wide].astype(F32) * up
            write = k * down * betas[h][of]
            offset = query_up * start_factor
            return (
                split(key_up)
                + split(query_up)
                + split(write)
                + split(key_up * start_factor)
                + split(write * end_factor)
                + split(offset)
            )

        t = strip_map(table)
        tables[h, n] = dict(key_offset=t[6:8], key_end=t[8:10], query_offset=t[10:12])
        ups = (jnp.concatenate([t[0], t[2]], axis=0), jnp.concatenate([t[1], t[3]], axis=0))
        both = nt(ups, t[4:6])

        def scores(at):
            below = slice(at.start + SPAN, at.stop + SPAN)
            keys = jnp.where(rows[at] > cols[at], both[at], 0.0)
            queries = jnp.where(rows[at] >= cols[at], both[below], 0.0)
            return whole_and_split(keys) + split(queries)

        t = strip_map(scores)
        strict[h, n] = t[:3]
        reach[h, n] = t[3:]
    inverses = dict(zip(places, unit_lower_inverses([strict[p] for p in places], mask_ref)))
    solved = {}
    for h, n in places:
        of = slice(n * SPAN, (n + 1) * SPAN)
        base = h * 4 * SPAN
        for i, x in enumerate(inverses[h, n] + reach[h, n]):
            ar_ref[of, base + i * SPAN : base + (i + 1) * SPAN] = x
        solved[h, n] = (
            nn(inverses[h, n], tables[h, n]["key_offset"]),
            nn(inverses[h, n], v_ref[of, h * DK : (h + 1) * DK]),
        )
    state, read = {}, {}
    for n in range(spans):
        for h in range(batch):
            t = tables[h, n]
            across, value = solved[h, n]
            base = n * SPAN
            of = slice(base, base + SPAN)
            wide = slice(h * DK, (h + 1) * DK)
            if n == 0:
                ux_map = strip_map(lambda at: split(-across[at]))
                shift = value
            else:
                across = split_strips(across)
                moved = nn(across, (state[h][1], state[h][2]))
                ux_map = strip_map(lambda at: split(-moved[at, :DK]))
                (shift,) = strip_map(lambda at: (value[at] - moved[at, DK:],))
            ux_shift = split_strips(shift)
            ub_ref[of, wide] = shift
            um_ref[of, h * 2 * DK : h * 2 * DK + DK] = ux_map[0]
            um_ref[of, h * 2 * DK + DK : (h + 1) * 2 * DK] = ux_map[1]
            through = nn(reach[h, n], ux_map)
            if n == 0:
                direct = whole(t["query_offset"])
            else:
                direct = nn(t["query_offset"], (state[h][1][:, :DK], state[h][2][:, :DK]))
            out_map = strip_map(lambda at: split(direct[at] + through[at]))
            added = tn(
                t["key_end"],
                tuple(jnp.concatenate([m, s], axis=1) for m, s in zip(ux_map, ux_shift)),
            )
            if n == 0:
                kept = jnp.concatenate([diagonal(finals[h, n]), jnp.zeros((DK, DV), F32)], axis=1)
                (new,) = strip_map(lambda at: (kept[at] + added[at],))
            else:
                factor = column(finals[h, n])
                (new,) = strip_map(lambda at: (factor[at] * state[h][0][at] + added[at],))
            state[h] = (new,) + (split_strips(new) if n < spans - 1 else ())
            term = tn(out_map, do_ref[of, wide])
            read[h] = term if n == 0 else read[h] + term
    for h in range(batch):
        slot = (jnp.bitwise_xor(swapped, h // own), h % own)
        store_message(msg_ref, slot, state[h][0][:, :DK], state[h][0][:, DK:], read[h])


def store_message(msg_ref, place, block_map, shift, read):
    rows, cols = iotas()
    left = None
    for i in range(0, DK, STRIP):
        at = slice(i, i + STRIP)
        rounded = block_map[at].astype(BF16)
        msg_ref[*place, at, :] = rounded
        part = jnp.where(rows[at] == cols[at], block_map[at] - rounded.astype(F32), 0.0)
        left = part if left is None else left + part
        msg_ref[*place, DK + i : DK + i + STRIP, :] = shift[at].astype(BF16)
        msg_ref[*place, 2 * DK + i : 2 * DK + i + STRIP, :] = read[at].astype(BF16)
    msg_ref[*place, 3 * DK :, :] = jnp.broadcast_to(
        jnp.sum(left, axis=0, keepdims=True), (16, DK)
    ).astype(BF16)


def load_map(ref, *at):
    rows, cols = iotas()
    row = ref[at + (slice(3 * DK, ROWS), slice(None))][0:1, :].astype(F32)
    return (
        ref[at + (slice(0, DK), slice(None))],
        jnp.where(rows == cols, row, 0.0).astype(BF16),
    )


def load_shift(ref, *at):
    return ref[at + (slice(DK, 2 * DK), slice(None))]


def load_read(ref, *at):
    return ref[at + (slice(2 * DK, 3 * DK), slice(None))]


def whole_map(parts):
    return parts[0].astype(F32) + parts[1].astype(F32)


def backward_kernel(batch, groups, group, q_ref, k_ref, g_ref, do_ref, beta_ref, ar_ref, wm_ref, wb_ref):
    step = pl.program_id(0) * groups + group
    spans = q_ref.shape[0] // SPAN
    betas = [head_betas(beta_ref, step * batch + h) for h in range(batch)]
    carried = {}
    for n in range(spans - 1, -1, -1):
        for h in range(batch):
            base = n * SPAN
            of = slice(base, base + SPAN)
            wide = slice(h * DK, (h + 1) * DK)
            running, middle, start_factor, end_factor, final = decays(g_ref[of, wide])

            def table(at):
                of = slice(base + at.start, base + at.stop)
                k = k_ref[of, wide].astype(F32)
                found = split(k * jnp.exp(middle - running[at]) * betas[h][of] * end_factor)
                if n > 0:
                    up = jnp.exp(running[at] - middle) * start_factor
                    found += split(k * up) + split(q_ref[of, wide].astype(F32) * up)
                return found

            t = strip_map(table)
            do = do_ref[of, wide]
            inverse, reach = [
                tuple(
                    ar_ref[of, (h * 4 + i) * SPAN : (h * 4 + i + 1) * SPAN] for i in (j, j + 1)
                )
                for j in (0, 2)
            ]
            own = tn(inverse, split_strips(tn(reach, do)))
            through = split_strips(tn(inverse, t[0:2]))
            if n == spans - 1:
                wx_map, shift = through, own
            else:
                moved = nn(through, carried[h][1:])
                wx_map = strip_map(lambda at: split(moved[at, :DK]))
                (shift,) = strip_map(lambda at: (moved[at, DK:] + own[at],))
            wb_ref[of, wide] = shift
            wm_ref[of, h * 2 * DK : h * 2 * DK + DK] = wx_map[0]
            wm_ref[of, h * 2 * DK + DK : (h + 1) * 2 * DK] = wx_map[1]
            if n > 0:
                wx_shift = split_strips(shift)
                taken = tn(t[2:4], tuple(jnp.concatenate([m, s], axis=1) for m, s in zip(wx_map, wx_shift)))
                read = tn(t[4:6], do)
                if n == spans - 1:
                    kept = diagonal(final)
                    (left,) = strip_map(lambda at: (kept[at] - taken[at, :DK],))
                    (right,) = strip_map(lambda at: (read[at] - taken[at, DK:],))
                else:
                    factor = column(final)
                    before = carried[h][0]
                    (left,) = strip_map(lambda at: (factor[at] * before[at, :DK] - taken[at, :DK],))
                    (right,) = strip_map(
                        lambda at: (factor[at] * before[at, DK:] + read[at] - taken[at, DK:],)
                    )
                new = jnp.concatenate([left, right], axis=1)
                carried[h] = (new,) + split_strips(new)


def compose_kernel(me_ref, parts_ref, total_ref):
    me = me_ref[0]
    count, heads = parts_ref.shape[:2]
    states, reads = [], []
    for h in range(heads):
        first = load_map(parts_ref, me, h)
        states.append(jnp.concatenate([whole_map(first), load_shift(parts_ref, me, h).astype(F32)], axis=1))
        reads.append(load_read(parts_ref, jnp.bitwise_xor(me, count - 1), h).astype(F32))
    for j in range(1, count):
        at = jnp.bitwise_xor(me, j)
        back = jnp.bitwise_xor(me, count - 1 - j)
        for h in range(heads):
            moved = nn(load_map(parts_ref, at, h), states[h])
            states[h] = jnp.concatenate(
                [moved[:, :DK], moved[:, DK:] + load_shift(parts_ref, at, h).astype(F32)], axis=1
            )
            reads[h] = tn(load_map(parts_ref, back, h), reads[h]) + load_read(parts_ref, back, h).astype(F32)
    for h in range(heads):
        store_message(total_ref, (h,), states[h][:, :DK], states[h][:, DK:], reads[h])


def join_kernel(first, upper_ref, own_ref, other_ref, carry_ref, total_ref, next_ref):
    heads = own_ref.shape[0]
    rows, cols = iotas()
    unit = jnp.where(rows == cols, 1.0, 0.0)

    def part(i):
        return slice(i * DK, (i + 1) * DK)

    @pl.when(upper_ref[0] == 1)
    def _():
        for h in range(heads):
            early = load_map(other_ref, h)
            shift = load_shift(other_ref, h)
            if first:
                next_ref[h, part(0)] = whole_map(early)
                next_ref[h, part(1)] = shift.astype(F32)
                next_ref[h, part(2)] = jnp.zeros((DK, DV), F32)
                next_ref[h, part(3)] = unit
            else:
                before = split(carry_ref[h, part(0)])
                next_ref[h, part(0)] = nn(before, early)
                next_ref[h, part(1)] = nn(before, shift) + carry_ref[h, part(1)]
                next_ref[h, part(2)] = carry_ref[h, part(2)]
                next_ref[h, part(3)] = carry_ref[h, part(3)]
            late = load_map(own_ref, h)
            store_message(
                total_ref,
                (h,),
                nn(late, early),
                nn(late, shift) + load_shift(own_ref, h).astype(F32),
                load_read(other_ref, h).astype(F32) + tn(early, load_read(own_ref, h)),
            )

    @pl.when(upper_ref[0] == 0)
    def _():
        for h in range(heads):
            late = load_map(other_ref, h)
            read = load_read(other_ref, h)
            if first:
                next_ref[h, part(0)] = unit
                next_ref[h, part(1)] = jnp.zeros((DK, DV), F32)
                next_ref[h, part(2)] = read.astype(F32)
                next_ref[h, part(3)] = whole_map(late)
            else:
                after = split(carry_ref[h, part(3)])
                next_ref[h, part(0)] = carry_ref[h, part(0)]
                next_ref[h, part(1)] = carry_ref[h, part(1)]
                next_ref[h, part(2)] = tn(after, read) + carry_ref[h, part(2)]
                next_ref[h, part(3)] = nn(late, after)
            early = load_map(own_ref, h)
            store_message(
                total_ref,
                (h,),
                nn(late, early),
                nn(late, load_shift(own_ref, h)) + load_shift(other_ref, h).astype(F32),
                load_read(own_ref, h).astype(F32) + tn(early, read),
            )


def spread_kernel(me_ref, upper_ref, other_ref, parts_ref, carry_ref, out_ref, ends_ref):
    me = me_ref[0]
    count, heads = parts_ref.shape[:2]
    ends_ref[...] = carry_ref[:, DK : 3 * DK]

    @pl.when(upper_ref[0] == 1)
    def _():
        for h in range(heads):
            ends_ref[h, 0:DK] = carry_ref[h, DK : 2 * DK] + nn(carry_ref[h, 0:DK], other_ref[h])

    @pl.when(upper_ref[0] == 0)
    def _():
        for h in range(heads):
            ends_ref[h, DK:] = carry_ref[h, 2 * DK : 3 * DK] + tn(carry_ref[h, 3 * DK :], other_ref[h])

    states = [ends_ref[h, 0:DK] for h in range(heads)]
    grads = [ends_ref[h, DK:] for h in range(heads)]
    for j in range(count):
        at = jnp.bitwise_xor(me, j)
        back = jnp.bitwise_xor(me, count - 1 - j)
        for h in range(heads):
            out_ref[at, h, 0:DK] = states[h].astype(BF16)
            out_ref[back, h, DK:] = grads[h].astype(BF16)
            if j < count - 1:
                states[h] = nn(load_map(parts_ref, at, h), states[h]) + load_shift(parts_ref, at, h).astype(F32)
                grads[h] = tn(load_map(parts_ref, back, h), grads[h]) + load_read(parts_ref, back, h).astype(F32)


def gradient_kernel(
    batch, groups, group, me_ref, q_ref, k_ref, g_ref, do_ref, beta_ref, um_ref, ub_ref, wm_ref, wb_ref, ends_ref,
    *refs,
):
    del me_ref
    dq_ref, dk_ref, dv_ref, dg_ref, db_ref = refs[-5:]
    step = pl.program_id(0) * groups + group
    tokens = q_ref.shape[0]
    spans = tokens // SPAN
    rows, cols = iotas()
    upper = jnp.where(rows <= cols, 1.0, 0.0).astype(BF16)
    ones = jnp.ones((8, DV), BF16)
    heads = lax.broadcasted_iota(jnp.int32, (beta_ref.shape[0], tokens), 0)

    @pl.when(pl.program_id(0) == 0)
    def _():
        db_ref[...] = refs[0][...] if group else jnp.zeros_like(db_ref)

    all_gates = db_ref[...].astype(F32)
    for h in range(batch):
        head = step * batch + h
        beta = head_betas(beta_ref, head)
        wide = slice(h * DK, (h + 1) * DK)
        high_half = slice(h * 2 * DK, h * 2 * DK + DK)
        low_half = slice(h * 2 * DK + DK, (h + 1) * 2 * DK)
        start = ends_ref[h, 0:DK]
        end = ends_ref[h, DK:]
        moved = nn((um_ref[:, high_half], um_ref[:, low_half]), start)
        written = strip_map(lambda at: split(ub_ref[at, wide] + moved[at]), tokens)
        back = nn((wm_ref[:, high_half], wm_ref[:, low_half]), end)

        def writes(at):
            x = wb_ref[at, wide] + back[at]
            dv_ref[at, wide] = x.astype(BF16)
            return split(-x)

        left = strip_map(writes, tokens)
        sums, tables, us, lefts = [], [], [], []
        for n in range(spans):
            base = n * SPAN
            of = slice(base, base + SPAN)
            running, middle, start_factor, end_factor, final = decays(g_ref[of, wide])
            sums.append((running, middle, start_factor, end_factor, final))

            def table(at):
                of = slice(base + at.start, base + at.stop)
                up = jnp.exp(running[at] - middle)
                k = k_ref[of, wide].astype(F32)
                key_up = k * up
                query_up = q_ref[of, wide].astype(F32) * up
                write = k * jnp.exp(middle - running[at]) * beta[of]
                found = split(key_up) + split(query_up) + split(write)
                found += split(write * end_factor) if n < spans - 1 else (None, None)
                if n > 0:
                    found += split(key_up * start_factor) + split(query_up * start_factor)
                return found

            tables.append(optional_strips(table))
            us.append(tuple(x[of] for x in written))
            lefts.append(tuple(x[of] for x in left))
        states, grads = [start], [None] * spans
        state = start.astype(F32)
        for n in range(spans - 1):
            factor = column(sums[n][4])
            added = tn(tables[n][6:8], us[n], True)
            t = strip_map(lambda at: whole_and_split(factor[at] * state[at] + added[at]))
            state = t[0]
            states.append(t[1:])
        grads[spans - 1] = end
        grad = end.astype(F32)
        for n in range(spans - 1, 0, -1):
            factor = column(sums[n][4])
            added = tn(tables[n][8:10], lefts[n], True)
            read = tn(tables[n][10:12], do_ref[n * SPAN : (n + 1) * SPAN, wide])
            t = strip_map(lambda at: whole_and_split(factor[at] * grad[at] + added[at] + read[at]))
            grad = t[0]
            grads[n - 1] = t[1:]
        gates = []
        for n in range(spans):
            base = n * SPAN
            t = tables[n]
            high, low = lefts[n]
            do = do_ref[base : base + SPAN, wide]
            left = (
                jnp.concatenate([high, do], axis=0),
                jnp.concatenate([low, jnp.zeros_like(low)], axis=0),
            )
            held = states[n] if isinstance(states[n], tuple) else (states[n], jnp.zeros_like(states[n]))
            met = nt(left, tuple(jnp.concatenate(x, axis=0) for x in zip(held, us[n])))
            grad_end = nt(us[n], grads[n])

            def masked(at):
                below = slice(at.start + SPAN, at.stop + SPAN)
                keys = jnp.where(rows[at] > cols[at], met[at, DK:], 0.0)
                queries = jnp.where(rows[at] >= cols[at], met[below, DK:], 0.0)
                return split(keys) + split(queries)

            pairs = strip_map(masked)
            pairs = tuple(jnp.concatenate([pairs[i], pairs[i + 2]], axis=0) for i in range(2))
            raised = nn(pairs, t[4:6])
            ups = tuple(jnp.concatenate([t[i], t[i + 2]], axis=0) for i in range(2))
            downs = tn(pairs, ups, True)
            running, middle, start_factor, end_factor, final = sums[n]
            last = [None]

            def finish(at):
                of = slice(base + at.start, base + at.stop)
                up = jnp.exp(running[at] - middle)
                down = jnp.exp(middle - running[at])
                k = k_ref[of, wide].astype(F32)
                q = q_ref[of, wide].astype(F32)
                below = slice(at.start + SPAN, at.stop + SPAN)
                query_part = (raised[below] + met[below, :DK] * start_factor) * up
                key_part = (raised[at] + met[at, :DK] * start_factor) * up
                gate_part = (downs[at] + grad_end[at] * end_factor) * down
                write_part = gate_part * beta[of]
                dq_ref[of, wide] = query_part.astype(BF16)
                dk_ref[of, wide] = (key_part + write_part).astype(BF16)
                term = grad_end[at] * (k * down * beta[of])
                last[0] = term if last[0] is None else last[0] + term
                return split(q * query_part + k * (key_part - write_part)) + split(gate_part * k)

            flow_high, flow_low, *gate = strip_map(finish)
            gates.append(nt(ones, tuple(gate))[0:1])
            state, grad = states[n], grads[n]
            held = strip_map(lambda at: split(whole_at(state, at) * whole_at(grad, at)))
            row = jnp.sum(last[0], axis=0, keepdims=True) * end_factor + final * nt(ones, held)[0:1]
            sums_back = nn(upper, (flow_high, flow_low))
            for i in range(0, SPAN, STRIP):
                dg_ref[base + i : base + i + STRIP, wide] = (sums_back[i : i + STRIP] + row).astype(BF16)
        gate = jnp.concatenate(gates, axis=1)
        all_gates = jnp.where(heads == head, gate, all_gates)
    db_ref[...] = all_gates.astype(BF16)


def whole_at(x, at):
    if isinstance(x, tuple):
        return x[0][at].astype(F32) + x[1][at].astype(F32)
    return x[at].astype(F32)


def optional_strips(fn):
    found = [fn(slice(i, i + STRIP)) for i in range(0, SPAN, STRIP)]
    return tuple(
        None if parts[0] is None else jnp.concatenate(parts, axis=0) for parts in zip(*found)
    )


def whole(x):
    if isinstance(x, tuple):
        return x[0].astype(F32) + x[1].astype(F32)
    return x.astype(F32)


def params(semantics=("arbitrary",)):
    return pltpu.CompilerParams(dimension_semantics=semantics, vmem_limit_bytes=56 << 20)


def cost(flops, data):
    return pl.CostEstimate(flops=int(flops), bytes_accessed=int(data), transcendentals=0)


def exchange(parts, axis):
    count = parts.shape[0]
    return jnp.stack(
        [parts[0]]
        + [lax.ppermute(parts[d], axis, [(i, i ^ d) for i in range(count)]) for d in range(1, count)]
    )


SMEM = pl.BlockSpec(memory_space=pltpu.SMEM)
VMEM = pl.BlockSpec(memory_space=pltpu.VMEM)
SMALL = pltpu.CompilerParams(vmem_limit_bytes=40 << 20)


class Group:
    def __init__(self, tokens, heads, count, groups, group):
        self.tokens, self.heads, self.count = tokens, heads, count
        self.batch = heads // count // groups
        self.ids = (self.batch, groups, group)
        self.groups, self.group = groups, group
        self.flops = 2 * 3 * count * self.batch * tokens * DK * DK
        self.beta = pl.BlockSpec((heads, tokens), lambda i, *_: (0, 0))

    def paired(self, place, pair):
        return pl.BlockSpec(
            (self.tokens, self.batch * DK),
            lambda i, *_: (0, (i * pair + place) * self.groups + self.group),
        )

    def wide(self):
        return pl.BlockSpec(
            (self.tokens, self.batch * DK), lambda i, *_: (0, i * self.groups + self.group)
        )

    def own(self, columns):
        return pl.BlockSpec((self.tokens, self.batch * columns), lambda i, *_: (0, i))

    def ordered(self, rows):
        return pl.BlockSpec(
            (None, self.batch, rows, DK), lambda i, m: (jnp.bitwise_xor(i, m[0]), 0, 0, 0)
        )

    def tables(self, columns, kind):
        return jax.ShapeDtypeStruct((self.tokens, self.count * self.batch * columns), kind)

    def block_maps(self, me, queries, key_rows, value_matrix, log_decay, grad_out, beta_gate):
        masks = level_masks()
        pair = 2 if self.groups > 1 and self.count % 2 == 0 else 1
        arrays = (queries, key_rows, value_matrix, log_decay, grad_out)

        def own(columns):
            return pl.BlockSpec((self.tokens, pair * self.batch * columns), lambda i, *_: (0, i))

        return pl.pallas_call(
            functools.partial(block_kernel, *self.ids, pair),
            grid_spec=pltpu.PrefetchScalarGridSpec(
                num_scalar_prefetch=1,
                grid=(self.count // pair,),
                in_specs=[self.paired(place, pair) for _ in arrays for place in range(pair)]
                + [self.beta, pl.BlockSpec(masks.shape, lambda i, *_: (0, 0, 0))],
                out_specs=[
                    pl.BlockSpec(
                        (pair, self.batch, ROWS, DK),
                        lambda i, m: (jnp.bitwise_xor(i, m[0] // pair), 0, 0, 0),
                    ),
                    own(2 * DK),
                    own(DK),
                    own(4 * SPAN),
                ],
            ),
            out_shape=[
                jax.ShapeDtypeStruct((self.count, self.batch, ROWS, DK), BF16),
                self.tables(2 * DK, BF16),
                self.tables(DK, F32),
                self.tables(4 * SPAN, BF16),
            ],
            compiler_params=params(),
            cost_estimate=cost(24 * self.flops, 20 << 20),
            name="block_maps",
        )(me, *[x for x in arrays for _ in range(pair)], beta_gate, masks)

    def backward_maps(self, queries, key_rows, log_decay, grad_out, beta_gate, ar):
        return pl.pallas_call(
            functools.partial(backward_kernel, *self.ids),
            grid_spec=pltpu.PrefetchScalarGridSpec(
                num_scalar_prefetch=0,
                grid=(self.count,),
                in_specs=[self.wide()] * 4 + [self.beta, self.own(4 * SPAN)],
                out_specs=[self.own(2 * DK), self.own(DK)],
            ),
            out_shape=[self.tables(2 * DK, BF16), self.tables(DK, F32)],
            compiler_params=params(),
            cost_estimate=cost(8 * self.flops, 12 << 20),
            name="backward_maps",
        )(queries, key_rows, log_decay, grad_out, beta_gate, ar)

    def compose(self, me, parts):
        return pl.pallas_call(
            compose_kernel,
            in_specs=[SMEM, VMEM],
            out_specs=VMEM,
            out_shape=jax.ShapeDtypeStruct((self.batch, ROWS, DK), BF16),
            compiler_params=SMALL,
            name="compose",
        )(me, parts)

    def join(self, first, upper, total, other, carry):
        return pl.pallas_call(
            functools.partial(join_kernel, first),
            in_specs=[SMEM, VMEM, VMEM, VMEM],
            out_specs=[VMEM, VMEM],
            out_shape=[
                jax.ShapeDtypeStruct((self.batch, ROWS, DK), BF16),
                jax.ShapeDtypeStruct((self.batch, 4 * DK, DK), F32),
            ],
            compiler_params=SMALL,
            name="join",
        )(upper, total, other, carry)

    def spread(self, me, upper, other, parts, carry):
        return pl.pallas_call(
            spread_kernel,
            in_specs=[SMEM, SMEM, VMEM, VMEM, VMEM],
            out_specs=VMEM,
            out_shape=jax.ShapeDtypeStruct((self.count, self.batch, 2 * DK, DV), BF16),
            scratch_shapes=[pltpu.VMEM((self.batch, 2 * DK, DV), F32)],
            compiler_params=SMALL,
            name="spread",
        )(me, upper, other, parts, carry)

    def gradients(self, me, queries, key_rows, log_decay, grad_out, beta_gate, ux, wx, ends, before):
        inputs = [self.wide()] * 4 + [self.beta] + [self.own(2 * DK), self.own(DK)] * 2 + [self.ordered(2 * DK)]
        aliases = {}
        extra = ()
        if before is not None:
            inputs = inputs + [self.beta] + [pl.BlockSpec(memory_space=pl.ANY)] * 4
            aliases = {12 + i: i for i in range(4)}
            extra = (before[4],) + tuple(before[:4])
        token_shape = jax.ShapeDtypeStruct(queries.shape, BF16)
        return pl.pallas_call(
            functools.partial(gradient_kernel, *self.ids),
            grid_spec=pltpu.PrefetchScalarGridSpec(
                num_scalar_prefetch=1,
                grid=(self.count,),
                in_specs=inputs,
                out_specs=[self.wide()] * 4 + [self.beta],
            ),
            out_shape=[token_shape] * 4 + [jax.ShapeDtypeStruct(beta_gate.shape, BF16)],
            input_output_aliases=aliases,
            compiler_params=params(),
            cost_estimate=cost(16 * self.flops, 20 << 20),
            name="gradients",
        )(me, queries, key_rows, log_decay, grad_out, beta_gate, *ux, *wx, ends, *extra)


GROUPS = 2


def local(queries, key_rows, value_matrix, log_decay, beta_gate, grad_out):
    tokens, heads = beta_gate.shape
    beta_gate = beta_gate.T
    count = lax.axis_size("head")
    blocks = lax.axis_size("seq")
    me = lax.axis_index("head").astype(jnp.int32).reshape(1)
    place = lax.axis_index("seq").astype(jnp.int32)
    groups = GROUPS if (heads // count) % GROUPS == 0 else 1
    work = [Group(tokens, heads, count, groups, i) for i in range(groups)]
    ids = range(groups)

    def upper(distance):
        return (jnp.bitwise_and(place, distance) != 0).astype(jnp.int32).reshape(1)

    def swap(x, distance):
        return lax.ppermute(x, "seq", [(i, i ^ distance) for i in range(blocks)])

    tables = [
        w.block_maps(me, queries, key_rows, value_matrix, log_decay, grad_out, beta_gate) for w in work
    ]
    gathered = [exchange(tables[i][0], "head") for i in ids]
    wx = [
        w.backward_maps(queries, key_rows, log_decay, grad_out, beta_gate, tables[i][3])
        for i, w in enumerate(work)
    ]
    totals = [w.compose(me, gathered[i]) for i, w in enumerate(work)]
    carries = [jnp.zeros((w.batch, 4 * DK, DK), F32) for w in work]
    distance = 1
    while 2 * distance < blocks:
        for i, w in enumerate(work):
            totals[i], carries[i] = w.join(
                distance == 1, upper(distance), totals[i], swap(totals[i], distance), carries[i]
            )
        distance *= 2
    high = upper(distance)
    outs = None
    for i, w in enumerate(work):
        sent = jnp.where(high[0] == 1, totals[i][:, 2 * DK : 3 * DK], totals[i][:, DK : 2 * DK])
        ends = w.spread(me, high, swap(sent, distance), gathered[i], carries[i])
        ends = exchange(ends, "head")
        outs = w.gradients(
            me, queries, key_rows, log_decay, grad_out, beta_gate, tables[i][1:3], wx[i], ends, outs
        )
    return *outs[:4], outs[4].T


def solution(mesh):
    spec = P(("seq", "head"), None)
    return jax.shard_map(
        lambda *arrays: tuple(local(*arrays)),
        mesh=mesh,
        in_specs=(spec,) * 6,
        out_specs=(spec,) * 5,
        check_vma=False,
    )
```
